32 devices in a mesh: groups: 2 (over y), expert: 4 (over z), tensor: 4 (over x, core).
Axes of the slice: x: 2, y: 2, z: 4, core: 2. Of those that a mesh axis runs over, the one named last changes fastest.
Arguments:
- tokens: bfloat16 [512, 7168], P(('groups', 'expert')), parts along dimension 0, may hold values from -6 to 6
- expert_ids: int32 [512, 2], P(('groups', 'expert')), parts along dimension 0, may hold values from 0 to 3, all different within a row; in each aligned block of 64 rows (0 to 63, 64 to 127, ...) at most 40 rows name the same one
- gate_scores: float32 [512, 2], P(('groups', 'expert')), parts along dimension 0, may hold values from 0.05 to 1
- w_gate: bfloat16 [4, 7168, 2048], P('expert', None, 'tensor'), may hold values from -0.0625 to 0.0625
- w_up: bfloat16 [4, 7168, 2048], P('expert', None, 'tensor'), may hold values from -0.0625 to 0.0625
- w_down: bfloat16 [4, 2048, 7168], P('expert', 'tensor'), may hold values from -0.1875 to 0.1875
Outputs:
- mixed: bfloat16 [512, 7168], P(('groups', 'expert'), 'tensor'), parts along dimension 0
The draws below stay inside these ranges and needn't reach their ends.
There are 2 independent parts, one for each index of `groups`. The reference program is written for one: setup_inputs(seed, part) draws one part's arguments, and reference() takes and returns one part's arrays. A program takes and returns all parts, laid end to end along the dimension named above; an argument that names none is the same for every part. Nothing has to cross between parts.
Inputs may be any that keep to these rules, and one draw needn't show every extreme that they name: `expert_ids`: each row names 2 different experts. Among the 64 rows of one aligned block no expert is named by more than 40 rows, and in every draw some expert is named by exactly 40 rows of some block.
All inputs are finite; a program needn't handle non-finite values.
Results may differ from the reference program's by a relative error of at most 0.015.
Values may be sent and summed in bfloat16 or wider, within the bound.
No kernel may reach another device: no remote copies, remote signals or barrier semaphores. Data moves between devices by JAX's collectives and lax.ppermute only.
A program may use at most 128 MiB of HBM per device.

```python
import math
import jax
import jax.numpy as jnp
import numpy as np
from jax import lax

D = 7168
FF = 2048
TOK_DEV = 64
EXPERTS = 4
TOP = 2
CAP = 40
TOKENS = 256
N_TENSOR = 4


def strengthened(drawn, own_key, source, target, blocks, factor):
    def block_of(dim):
        return (jnp.arange(drawn.shape[dim]) // (drawn.shape[dim] // blocks)).reshape((-1,) + (1,) * (drawn.ndim - 1 - dim))

    first = jax.random.permutation(own_key, blocks)[block_of(target)]
    far = (block_of(target) + blocks // 2) % blocks
    return jnp.where((block_of(source) == first) | (block_of(source) == far), factor * drawn, drawn)


def level_of(rng, shape, pieces, low, top_value):
    gain, own = 1.0, jax.random.fold_in(rng, 6)
    for axis_at, parts in pieces:
        draws = jnp.exp(jax.random.uniform(jax.random.fold_in(own, axis_at), (parts,), jnp.float32, low / len(pieces), top_value / len(pieces)))
        gain = gain * jnp.repeat(draws, shape[axis_at] // parts).reshape([-1 if axis == axis_at else 1 for axis in range(len(shape))])
    return gain


def assign_block(own_key, own, number, rows, number_of, top, bound, lean):
    sequence = jax.random.permutation(own_key, number_of)
    crowded, ordinary = portions_of(number_of, rows * top, bound, lean, True), portions_of(number_of, rows * top, bound, lean, False)
    places = jnp.arange(number_of)

    def named(lengths, offset_by):
        used = int((lengths > 0).sum())
        fixed = max(1, used // 4)
        passed = fixed + (places - fixed + offset_by * (used - fixed)) % max(1, number_of - fixed)
        return jnp.zeros((number_of,), jnp.int32).at[sequence[jnp.where(places < fixed, places, passed)]].set(jnp.asarray(lengths, jnp.int32))

    lengths = jnp.where(number % 4 == 0, named(crowded, number // 4), named(ordinary, number - number // 4 - 1))
    mixed = jax.random.permutation(jax.random.fold_in(own, 3), number_of)
    donor, taker = mixed[0:number_of // 2 * 2:2], mixed[1:number_of // 2 * 2:2]
    room = jnp.minimum(lengths[donor] - 1, bound - lengths[taker]) // 2
    room = jnp.where((donor == sequence[0]) | (taker == sequence[0]) | (lengths[taker] == 0), 0, jnp.maximum(room, 0))
    passed = jax.random.randint(jax.random.fold_in(own, 4), (number_of // 2,), 0, 1 << 20) % (room + 1)
    lengths = lengths.at[donor].add(-passed).at[taker].add(passed)
    members = jnp.searchsorted(jnp.cumsum(lengths), jnp.arange(rows * top), side="right").astype(jnp.int32)
    listing = members.reshape(top, rows).T
    listing = listing[jax.random.permutation(jax.random.fold_in(own, 1), rows)]
    offset_by = jax.random.randint(jax.random.fold_in(own, 2), (rows, 1), 0, top)
    return jnp.take_along_axis(listing, (jnp.arange(top)[None, :] + offset_by) % top, axis=1)


def portions_of(count, total, limit, slope, full):
    weights = [(1 << 20) // math.isqrt(standing ** slope) + 1 for standing in range(1, count + 1)]
    largest = limit if full else min(limit, max(-(-total // count), total * weights[0] // sum(weights)))
    least = 1 if total - largest >= count - 1 else 0
    given, surplus = [largest] + [least] * (count - 1), total - largest - least * (count - 1)
    while surplus > 0:
        candidates = [i for i in range(1, count) if given[i] < largest] or [i for i in range(1, count) if given[i] < limit]
        whole, budget = sum([weights[i] for i in candidates]), surplus
        for i in candidates:
            addition = min(limit - given[i], max(1, budget * weights[i] // whole), surplus)
            given[i] = given[i] + addition
            surplus = surplus - addition
    return np.array(given)


def normal_values(own_key, extent, deviation, reach, pieces=(), held_as=jnp.bfloat16):
    drawn = deviation * jax.random.normal(own_key, extent, jnp.float32)
    if pieces:
        drawn = drawn * level_of(own_key, extent, pieces, -0.22, 0.18)
    return jnp.clip(drawn, -reach, reach).astype(held_as)


def gaussian_with(stream_key, dims, scale, bound, shards, heavy, held_as=jnp.bfloat16):
    array = scale * jax.random.normal(stream_key, dims, jnp.float32)
    if shards:
        array = array * level_of(stream_key, dims, shards, -0.22, 0.18)
    return jnp.clip(strengthened(array, jax.random.fold_in(stream_key, 3), *heavy), -bound, bound).astype(held_as)


def setup_inputs(seed: int = 0, part: int = 0) -> dict:
    keys = jax.random.split(jax.random.key(seed), 7)
    part_keys = jax.random.split(jax.random.fold_in(keys[6], part), 7)
    tokens = normal_values(part_keys[0], (TOKENS, D), 1.0, 6.0, ((0, 4),))
    expert_ids_keys = jax.random.split(jax.random.fold_in(part_keys[1], 1), TOKENS // TOK_DEV)
    expert_ids_turns = jax.random.permutation(jax.random.fold_in(part_keys[1], 3), TOKENS // TOK_DEV)
    expert_ids = jax.vmap(lambda own, number: assign_block(jax.random.fold_in(part_keys[1], 2), own, number, TOK_DEV, EXPERTS, TOP, CAP, 2))(expert_ids_keys, expert_ids_turns).reshape((TOKENS, TOP))
    gate_scores = jnp.clip(jnp.exp(math.log(1.0) - 2.9957323 * jax.random.uniform(part_keys[2], (TOKENS, TOP), jnp.float32) ** level_of(part_keys[2], (TOKENS, TOP), ((0, 4),), -0.2, 0.2)), 0.05, 1.0)
    w_gate = normal_values(keys[3], (EXPERTS, D, FF), D ** -0.5, 0.0625, ((0, 4), (2, 4)))
    w_up = normal_values(keys[4], (EXPERTS, D, FF), D ** -0.5, 0.0625, ((0, 4), (2, 4)))
    w_down = gaussian_with(keys[5], (EXPERTS, FF, D), FF ** -0.5, 0.1875, ((0, 4), (1, 4)), (1, 2, 4, 2.0))
    return dict(tokens=tokens, expert_ids=expert_ids, gate_scores=gate_scores, w_gate=w_gate, w_up=w_up, w_down=w_down)


def slot_table(expert_ids, experts, capacity):
    tok_rows = expert_ids.shape[0]
    chosen = jnp.sum(jax.nn.one_hot(expert_ids, experts, dtype=jnp.int32), axis=1)
    before = jnp.cumsum(chosen, axis=0) - chosen
    position = jnp.take_along_axis(before, expert_ids, axis=1)
    slot_ids = (expert_ids * capacity + position).astype(jnp.int32)
    all_slots = jnp.arange(experts * capacity, dtype=jnp.int32)
    matches = (slot_ids[:, :, None] == all_slots[None, None, :]).astype(jnp.int32)
    filled = jnp.sum(matches, axis=(0, 1))
    token_index = jnp.arange(tok_rows, dtype=jnp.int32)
    source = jnp.sum(matches * token_index[:, None, None], axis=(0, 1)).astype(jnp.int32)
    return slot_ids, source, filled


def reference(tokens, expert_ids, gate_scores, w_gate, w_up, w_down):
    experts = EXPERTS
    capacity = CAP
    width = D
    groups = N_TENSOR
    block_ids = expert_ids.reshape(experts, TOK_DEV, TOP)
    block_tokens = tokens.reshape(experts, TOK_DEV, width)
    slot_ids, source, filled = jax.vmap(lambda ids: slot_table(ids, experts, capacity))(block_ids)

    def fill_block(block_rows, block_source, block_filled):
        return jnp.where((block_filled > 0)[:, None], block_rows[block_source], jnp.zeros((), block_rows.dtype))

    buffers = jax.vmap(fill_block)(block_tokens, source, filled)
    per_expert = buffers.reshape(experts, experts, capacity, width).transpose(1, 0, 2, 3)
    per_expert = per_expert.reshape(experts, experts * capacity, width)

    def run_expert(operands):
        inputs, gate_mat, up_mat, down_mat = operands
        gate_out = jnp.dot(inputs, gate_mat, preferred_element_type=jnp.float32)
        up_out = jnp.dot(inputs, up_mat, preferred_element_type=jnp.float32)
        hidden = (jax.nn.silu(gate_out) * up_out).astype(jnp.bfloat16)
        hidden_groups = hidden.reshape(-1, groups, FF // groups).astype(jnp.float32)
        down_groups = down_mat.reshape(groups, FF // groups, width).astype(jnp.float32)
        partial_value = jnp.einsum("rgf,gfd->grd", hidden_groups, down_groups).astype(jnp.bfloat16)
        partial_value = lax.optimization_barrier(partial_value).astype(jnp.float32)
        return jnp.sum(partial_value, axis=0).astype(jnp.bfloat16)

    outputs = lax.map(run_expert, (per_expert, w_gate, w_up, w_down))
    tables = outputs.reshape(experts, experts, capacity, width).transpose(1, 0, 2, 3)
    tables = tables.reshape(experts, experts * capacity, width)
    picked = jax.vmap(lambda table, slots: table[slots])(tables, slot_ids).astype(jnp.float32)
    weights = 2.5 * gate_scores / jnp.sum(gate_scores, axis=1, keepdims=True)
    weights = weights.reshape(experts, TOK_DEV, TOP)
    mixed = jnp.sum(weights[:, :, :, None] * picked, axis=2)
    return mixed.reshape(TOKENS, width).astype(jnp.bfloat16)
```

```python
import jax
import jax.numpy as jnp
from jax import lax
from jax.experimental import pallas as pl
from jax.experimental.pallas import tpu as pltpu
from jax.sharding import PartitionSpec as P

F32 = jnp.float32
BF16 = jnp.bfloat16
VMEM = pl.BlockSpec(memory_space=pltpu.VMEM)
HBM = pl.BlockSpec(memory_space=pl.ANY)


def params(limit_mib):
    return pltpu.CompilerParams(vmem_limit_bytes=limit_mib << 20)


def xor_permute(value, axis, step):
    size = lax.axis_size(axis)
    return lax.ppermute(value, axis, [(i, i ^ step) for i in range(size)])


def slot_rows(ids_ref, experts, me):
    top_k, rows = ids_ref.shape
    wanted = lax.broadcasted_iota(jnp.int32, (experts, rows), 0) ^ me
    chosen = jnp.zeros((experts, rows), F32)
    for k in range(top_k):
        chosen = chosen + (ids_ref[k : k + 1, :] == wanted).astype(F32)
    earlier = lax.broadcasted_iota(jnp.int32, (rows, rows), 0) < lax.broadcasted_iota(
        jnp.int32, (rows, rows), 1
    )
    before = jnp.dot(
        chosen.astype(BF16), earlier.astype(BF16), preferred_element_type=F32
    )
    return chosen, before


def pick_matrix(chosen, before, step, capacity):
    rows = chosen.shape[1]
    slot = lax.broadcasted_iota(jnp.int32, (capacity, rows), 0).astype(F32)
    hit = (before[step : step + 1, :] == slot) & (chosen[step : step + 1, :] > 0)
    return hit.astype(F32).astype(BF16)


def build_kernel(steps, experts, capacity, ids_ref, tok_ref, *outs):
    me = lax.axis_index("expert")
    own = lax.axis_index("tensor")
    chosen, before = slot_rows(ids_ref, experts, me)
    for step, out in zip(steps, outs):
        matrix = pick_matrix(chosen, before, step, capacity)
        if step == 0:
            moved = jnp.dot(matrix, tok_ref[...], preferred_element_type=F32)
        else:
            sliver = out.shape[1]
            start = pl.multiple_of(own * sliver, 128)
            moved = jnp.dot(
                matrix, tok_ref[:, pl.ds(start, sliver)], preferred_element_type=F32
            )
        out[...] = moved.astype(out.dtype)


def build(ids_t, tokens, steps, experts, capacity, sliver):
    rows, width = tokens.shape
    shapes = [
        jax.ShapeDtypeStruct((capacity, width if s == 0 else sliver), tokens.dtype)
        for s in steps
    ]

    def kernel(*refs):
        build_kernel(steps, experts, capacity, *refs)

    return pl.pallas_call(
        kernel,
        out_shape=shapes,
        in_specs=[VMEM, VMEM],
        out_specs=[VMEM] * len(shapes),
        compiler_params=params(8),
        name="build_" + "_".join(str(s) for s in steps),
    )(ids_t, tokens)


def down_slivers(hidden, down_ref, sent_refs, kept_ref):
    own = lax.axis_index("tensor")
    sent_ref = sent_refs
    sliver = kept_ref.shape[-1]
    for j in range(2 * kept_ref.shape[0]):
        start = pl.multiple_of((own ^ j) * sliver, 128)
        part = jnp.dot(
            hidden, down_ref[:, pl.ds(start, sliver)], preferred_element_type=F32
        )
        if j % 2 == 1:
            sent_ref[j // 2] = part.astype(BF16)
        else:
            kept_ref[j // 2] = part


def activate(gate, up):
    return (gate / (1.0 + jnp.exp(-gate)) * up).astype(BF16)


def first_kernel(parts, rows_ref, gate_hbm, up_hbm, down_hbm, gate_ref, up_ref, down_ref, sent_ref, kept_ref, sems):
    depth = gate_ref.shape[0] // parts
    cols = down_ref.shape[1] // parts
    gate_copies, up_copies, down_copies = [], [], []
    for p in range(parts):
        at = pl.ds(p * depth, depth)
        gate_copies.append(pltpu.make_async_copy(gate_hbm.at[at], gate_ref.at[at], sems.at[p]))
        up_copies.append(pltpu.make_async_copy(up_hbm.at[at], up_ref.at[at], sems.at[parts + p]))
    rows_down = down_ref.shape[0] // parts
    for p in range(parts):
        at = pl.ds(p * rows_down, rows_down)
        down_copies.append(pltpu.make_async_copy(down_hbm.at[at], down_ref.at[at], sems.at[2 * parts + p]))
    for p in range(parts):
        gate_copies[p].start()
        up_copies[p].start()
    for p in range(parts):
        down_copies[p].start()
    gate = up = None
    for p in range(parts):
        at = pl.ds(p * depth, depth)
        lhs = rows_ref[:, at]
        gate_copies[p].wait()
        term = jnp.dot(lhs, gate_ref[at, :], preferred_element_type=F32)
        gate = term if gate is None else gate + term
        up_copies[p].wait()
        term = jnp.dot(lhs, up_ref[at, :], preferred_element_type=F32)
        up = term if up is None else up + term
    hidden = activate(gate, up)
    for p in range(parts):
        down_copies[p].wait()
    down_slivers(hidden, down_ref, sent_ref, kept_ref)


def first_pass(rows, gate_mat, up_mat, down_mat, slivers):
    count, width = rows.shape
    parts = 4
    sliver = width // slivers
    half = slivers // 2

    def kernel(*refs):
        first_kernel(parts, *refs)

    return pl.pallas_call(
        kernel,
        out_shape=[
            jax.ShapeDtypeStruct(gate_mat.shape, BF16),
            jax.ShapeDtypeStruct(up_mat.shape, BF16),
            jax.ShapeDtypeStruct(down_mat.shape, BF16),
            jax.ShapeDtypeStruct((half, count, sliver), BF16),
            jax.ShapeDtypeStruct((half, count, sliver), F32),
        ],
        in_specs=[VMEM, HBM, HBM, HBM],
        out_specs=[VMEM] * 5,
        scratch_shapes=[pltpu.SemaphoreType.DMA((3 * parts,))],
        compiler_params=params(8),
        name="first_pass",
    )(rows, gate_mat, up_mat, down_mat)


def later_kernel(chunks, slivers, *refs):
    taken = chunks * slivers
    pieces = refs[:taken]
    gate_ref, up_ref, down_ref, sent_ref, kept_ref, lhs = refs[taken:]
    own = lax.axis_index("tensor")
    capacity, sliver = pieces[0].shape
    for c in range(chunks):
        for j in range(slivers):
            start = pl.multiple_of((own ^ j) * sliver, 128)
            lhs[pl.ds(c * capacity, capacity), pl.ds(start, sliver)] = pieces[c * slivers + j][...]
    gate = jnp.dot(lhs[...], gate_ref[...], preferred_element_type=F32)
    up = jnp.dot(lhs[...], up_ref[...], preferred_element_type=F32)
    down_slivers(activate(gate, up), down_ref, sent_ref, kept_ref)


def later_pass(pieces, weights, slivers):
    chunks = len(pieces)
    capacity, sliver = pieces[0][0].shape
    half = slivers // 2
    flat = [piece for chunk in pieces for piece in chunk]

    def kernel(*refs):
        later_kernel(chunks, slivers, *refs)

    count = chunks * capacity
    return pl.pallas_call(
        kernel,
        out_shape=[
            jax.ShapeDtypeStruct((half, count, sliver), BF16),
            jax.ShapeDtypeStruct((half, count, sliver), F32),
        ],
        in_specs=[VMEM] * (len(flat) + 3),
        out_specs=[VMEM] * 2,
        scratch_shapes=[pltpu.VMEM((count, sliver * slivers), BF16)],
        compiler_params=params(8),
        name="later_pass",
    )(*flat, *weights)


def combine_kernel(capacity, ids_ref, score_ref, *refs):
    tables, out_ref = refs[:-1], refs[-1]
    me = lax.axis_index("expert")
    rows, top_k = ids_ref.shape
    experts = len(tables)
    scores = score_ref[...]
    weights = 2.5 * scores / jnp.sum(scores, axis=1, keepdims=True)
    wanted = lax.broadcasted_iota(jnp.int32, (rows, experts), 1) ^ me
    chosen = jnp.zeros((rows, experts), F32)
    factor = jnp.zeros((rows, experts), F32)
    for k in range(top_k):
        hit = (ids_ref[:, k : k + 1] == wanted).astype(F32)
        chosen = chosen + hit
        factor = factor + hit * weights[:, k : k + 1]
    earlier = lax.broadcasted_iota(jnp.int32, (rows, rows), 1) < lax.broadcasted_iota(
        jnp.int32, (rows, rows), 0
    )
    before = jnp.dot(earlier.astype(BF16), chosen.astype(BF16), preferred_element_type=F32)
    slot = lax.broadcasted_iota(jnp.int32, (rows, capacity), 1).astype(F32)
    total = jnp.zeros(out_ref.shape, F32)
    for step, table in enumerate(tables):
        hit = (before[:, step : step + 1] == slot) & (chosen[:, step : step + 1] > 0)
        picked = jnp.dot(hit.astype(F32).astype(BF16), table[...], preferred_element_type=F32)
        total = total + factor[:, step : step + 1] * picked
    out_ref[...] = total.astype(out_ref.dtype)


def combine(ids, scores, tables):
    rows = ids.shape[0]
    capacity, sliver = tables[0].shape

    def kernel(*refs):
        combine_kernel(capacity, *refs)

    return pl.pallas_call(
        kernel,
        out_shape=jax.ShapeDtypeStruct((rows, sliver), BF16),
        in_specs=[VMEM] * (2 + len(tables)),
        out_specs=VMEM,
        compiler_params=params(8),
        name="combine",
    )(ids, scores, *tables)


def gather_slivers(piece, slivers):
    held = {0: piece}
    bits = [b for b in range(slivers.bit_length() - 1)]
    for bit in reversed(bits):
        step = 1 << bit
        for j in list(held):
            held[j ^ step] = xor_permute(held[j], "tensor", step)
    return [held[j] for j in range(slivers)]


def reduce_slivers(sent, kept, slivers):
    step = 1
    while True:
        arrived = xor_permute(sent, "tensor", step)
        total = kept + arrived.astype(F32)
        step *= 2
        if step == slivers:
            return total[0].astype(BF16)
        sent = total[1::2].astype(BF16)
        kept = total[0::2]


def per_device(tokens, expert_ids, gate_scores, w_gate, w_up, w_down):
    tok_rows, width = tokens.shape
    top_k = expert_ids.shape[1]
    experts = lax.axis_size("expert")
    slivers = lax.axis_size("tensor")
    capacity = 8 * ((5 * tok_rows * top_k // (4 * experts) + 7) // 8)
    sliver = width // slivers
    ids_t = expert_ids.T
    order = list(range(experts - 1, 0, -1))
    outs = build(ids_t, tokens, [*order, 0], experts, capacity, sliver)
    built = dict(zip([*order, 0], outs))
    arrived = {s: xor_permute(built[s], "expert", s) for s in order}
    *weights, sent, kept = first_pass(built[0], w_gate[0], w_up[0], w_down[0], slivers)
    tables = {0: reduce_slivers(sent, kept, slivers)}
    for s in order:
        pieces = gather_slivers(arrived[s], slivers)
        sent, kept = later_pass([pieces], weights, slivers)
        tables[s] = xor_permute(reduce_slivers(sent, kept, slivers), "expert", s)
    return combine(expert_ids, gate_scores, [tables[s] for s in range(experts)])


def solution(mesh):
    in_specs = (
        P(("groups", "expert"), None),
        P(("groups", "expert"), None),
        P(("groups", "expert"), None),
        P("expert", None, "tensor"),
        P("expert", None, "tensor"),
        P("expert", "tensor", None),
    )
    out_specs = P(("groups", "expert"), "tensor")
    return jax.shard_map(
        per_device, mesh=mesh, in_specs=in_specs, out_specs=out_specs, check_vma=False
    )
```

```python
import jax
import jax.numpy as jnp
from jax import lax
from jax.experimental import pallas as pl
from jax.experimental.pallas import tpu as pltpu
from jax.sharding import PartitionSpec as P

F32 = jnp.float32
BF16 = jnp.bfloat16
VMEM = pl.BlockSpec(memory_space=pltpu.VMEM)
HBM = pl.BlockSpec(memory_space=pl.ANY)
COST = pl.CostEstimate(flops=1000, bytes_accessed=1000, transcendentals=0)


def params(limit_mib):
    return pltpu.CompilerParams(vmem_limit_bytes=limit_mib << 20)


def xor_permute(value, axis, step):
    size = lax.axis_size(axis)
    return lax.ppermute(value, axis, [(i, i ^ step) for i in range(size)])


def slot_rows(ids_ref, experts, me):
    top_k, rows = ids_ref.shape
    wanted = lax.broadcasted_iota(jnp.int32, (experts, rows), 0) ^ me
    chosen = jnp.zeros((experts, rows), F32)
    for k in range(top_k):
        chosen = chosen + (ids_ref[k : k + 1, :] == wanted).astype(F32)
    earlier = lax.broadcasted_iota(jnp.int32, (rows, rows), 0) < lax.broadcasted_iota(
        jnp.int32, (rows, rows), 1
    )
    before = jnp.dot(
        chosen.astype(BF16), earlier.astype(BF16), preferred_element_type=F32
    )
    return chosen, before


def pick_matrix(chosen, before, step, capacity):
    rows = chosen.shape[1]
    slot = lax.broadcasted_iota(jnp.int32, (capacity, rows), 0).astype(F32)
    hit = (before[step : step + 1, :] == slot) & (chosen[step : step + 1, :] > 0)
    return hit.astype(F32).astype(BF16)


def build_kernel(steps, experts, capacity, ids_ref, tok_ref, *outs):
    me = lax.axis_index("expert")
    own = lax.axis_index("tensor")
    chosen, before = slot_rows(ids_ref, experts, me)
    for step, out in zip(steps, outs):
        matrix = pick_matrix(chosen, before, step, capacity)
        if step == 0:
            moved = jnp.dot(matrix, tok_ref[...], preferred_element_type=F32)
        else:
            sliver = out.shape[1]
            start = pl.multiple_of(own * sliver, 128)
            moved = jnp.dot(
                matrix, tok_ref[:, pl.ds(start, sliver)], preferred_element_type=F32
            )
        out[...] = moved.astype(out.dtype)


def build(ids_t, tokens, steps, experts, capacity, sliver):
    rows, width = tokens.shape
    shapes = [
        jax.ShapeDtypeStruct((capacity, width if s == 0 else sliver), tokens.dtype)
        for s in steps
    ]

    def kernel(*refs):
        build_kernel(steps, experts, capacity, *refs)

    return pl.pallas_call(
        kernel,
        out_shape=shapes,
        in_specs=[VMEM, VMEM],
        out_specs=[VMEM] * len(shapes),
        compiler_params=params(8),
        name="build_" + "_".join(str(s) for s in steps),
    )(ids_t, tokens)


def down_slivers(hidden, held_ref, sent_ref, kept_ref):
    own = lax.axis_index("tensor")
    strip = hidden.shape[1] // 2
    half, _, sliver = kept_ref.shape
    base = held_ref.shape[0] - 2 * half * sliver
    for j in range(2 * half):
        for c in range(sliver // strip):
            at = pl.multiple_of(base + (own ^ j) * sliver + c * strip, 128)
            part = jnp.dot(
                hidden[:, :strip], held_ref[pl.ds(at, strip), :strip], preferred_element_type=F32
            ) + jnp.dot(
                hidden[:, strip:], held_ref[pl.ds(at, strip), strip:], preferred_element_type=F32
            )
            if j % 2 == 1:
                sent_ref[j // 2, :, c * strip : (c + 1) * strip] = part.astype(BF16)
            else:
                kept_ref[j // 2, :, c * strip : (c + 1) * strip] = part


def activate(gate, up):
    return (gate / (1.0 + jnp.exp(-gate)) * up).astype(BF16)


def first_kernel(parts, rows_ref, gate_hbm, up_hbm, down_hbm, held_ref, sent_ref, kept_ref, sems):
    width, units = gate_hbm.shape
    strip = units // 2
    depth = width // parts

    def down_copies(p):
        copies = []
        for i in range(p * (width // strip) // parts, (p + 1) * (width // strip) // parts):
            for h in range(2):
                copies.append(
                    pltpu.make_async_copy(
                        down_hbm.at[pl.ds(h * strip, strip), pl.ds(i * strip, strip)],
                        held_ref.at[pl.ds(2 * width + i * strip, strip), pl.ds(h * strip, strip)],
                        sems.at[2 * parts + p],
                    )
                )
        return copies

    projections = []
    for p in range(parts):
        at = pl.ds(p * depth, depth)
        for which, source in enumerate((gate_hbm, up_hbm)):
            target = held_ref.at[pl.ds(which * width + p * depth, depth)]
            copy = pltpu.make_async_copy(source.at[at], target, sems.at[2 * p + which])
            copy.start()
            projections.append(copy)
    downs = [down_copies(p) for p in range(parts)]
    for copies in downs:
        for copy in copies:
            copy.start()
    sums = [None, None]
    for p in range(parts):
        lhs = rows_ref[:, p * depth : (p + 1) * depth]
        for which in range(2):
            projections[2 * p + which].wait()
            term = jnp.dot(
                lhs, held_ref[pl.ds(which * width + p * depth, depth), :], preferred_element_type=F32
            )
            sums[which] = term if p == 0 else sums[which] + term
    hidden = activate(*sums)
    for copies in downs:
        for copy in copies:
            copy.wait()
    down_slivers(hidden, held_ref, sent_ref, kept_ref)


def first_pass(rows, gate_mat, up_mat, down_mat, slivers):
    count, width = rows.shape
    parts = 4
    sliver = width // slivers
    half = slivers // 2
    units = gate_mat.shape[1]

    def kernel(*refs):
        first_kernel(parts, *refs)

    return pl.pallas_call(
        kernel,
        out_shape=[
            pltpu.VMEM((3 * width, units), BF16),
            jax.ShapeDtypeStruct((half, count, sliver), BF16),
            jax.ShapeDtypeStruct((half, count, sliver), F32),
        ],
        in_specs=[VMEM, HBM, HBM, HBM],
        out_specs=[VMEM] * 3,
        scratch_shapes=[pltpu.SemaphoreType.DMA((3 * parts,))],
        compiler_params=params(36),
        cost_estimate=COST,
        name="first_pass",
    )(rows, gate_mat, up_mat, down_mat)


def later_kernel(chunks, slivers, *refs):
    taken = chunks * slivers
    pieces = refs[:taken]
    held_ref, sent_ref, kept_ref, lhs = refs[taken:]
    own = lax.axis_index("tensor")
    capacity, sliver = pieces[0].shape
    width = sliver * slivers
    for c in range(chunks):
        for j in range(slivers):
            start = pl.multiple_of((own ^ j) * sliver, 128)
            lhs[pl.ds(c * capacity, capacity), pl.ds(start, sliver)] = pieces[c * slivers + j][...]
    gate = jnp.dot(lhs[...], held_ref[:width, :], preferred_element_type=F32)
    up = jnp.dot(lhs[...], held_ref[width : 2 * width, :], preferred_element_type=F32)
    down_slivers(activate(gate, up), held_ref, sent_ref, kept_ref)


def later_pass(pieces, held, slivers):
    chunks = len(pieces)
    capacity, sliver = pieces[0][0].shape
    half = slivers // 2
    flat = [piece for chunk in pieces for piece in chunk]

    def kernel(*refs):
        later_kernel(chunks, slivers, *refs)

    count = chunks * capacity
    return pl.pallas_call(
        kernel,
        out_shape=[
            jax.ShapeDtypeStruct((half, count, sliver), BF16),
            jax.ShapeDtypeStruct((half, count, sliver), F32),
        ],
        in_specs=[VMEM] * (len(flat) + 1),
        out_specs=[VMEM] * 2,
        scratch_shapes=[pltpu.VMEM((count, sliver * slivers), BF16)],
        compiler_params=params(8),
        cost_estimate=COST,
        name="later_pass",
    )(*flat, pltpu.with_memory_space_constraint(held, pltpu.VMEM))


def combine_kernel(capacity, ids_ref, score_ref, *refs):
    tables, out_ref = refs[:-1], refs[-1]
    me = lax.axis_index("expert")
    top_k, rows = ids_ref.shape
    experts = len(tables)
    chosen, before = slot_rows(ids_ref, experts, me)
    scores = score_ref[...]
    weights = 2.5 * scores / jnp.sum(scores, axis=0, keepdims=True)
    wanted = lax.broadcasted_iota(jnp.int32, (experts, rows), 0) ^ me
    factor = jnp.zeros((experts, rows), F32)
    for k in range(top_k):
        hit = (ids_ref[k : k + 1, :] == wanted).astype(F32)
        factor = factor + hit * weights[k : k + 1, :]
    factor = factor.T
    total = jnp.zeros(out_ref.shape, F32)
    for step, table in enumerate(tables):
        matrix = pick_matrix(chosen, before, step, capacity)
        picked = lax.dot_general(
            matrix, table[...], (((0,), (0,)), ((), ())), preferred_element_type=F32
        )
        total = total + factor[:, step : step + 1] * picked
    out_ref[...] = total.astype(out_ref.dtype)


def combine(ids_t, scores_t, tables):
    rows = ids_t.shape[1]
    capacity, sliver = tables[0].shape

    def kernel(*refs):
        combine_kernel(capacity, *refs)

    return pl.pallas_call(
        kernel,
        out_shape=jax.ShapeDtypeStruct((rows, sliver), BF16),
        in_specs=[VMEM] * (2 + len(tables)),
        out_specs=VMEM,
        compiler_params=params(8),
        name="combine",
    )(ids_t, scores_t, *tables)


def gather_slivers(piece, slivers):
    held = {0: piece}
    bits = [b for b in range(slivers.bit_length() - 1)]
    for bit in reversed(bits):
        step = 1 << bit
        for j in list(held):
            held[j ^ step] = xor_permute(held[j], "tensor", step)
    return [held[j] for j in range(slivers)]


def reduce_slivers(sent, kept, slivers):
    step = 1
    while True:
        arrived = xor_permute(sent, "tensor", step)
        total = kept + arrived.astype(F32)
        step *= 2
        if step == slivers:
            return total[0].astype(BF16)
        sent = total[1::2].astype(BF16)
        kept = total[0::2]


def per_device(tokens, expert_ids, gate_scores, w_gate, w_up, w_down):
    tok_rows, width = tokens.shape
    top_k = expert_ids.shape[1]
    experts = lax.axis_size("expert")
    slivers = lax.axis_size("tensor")
    capacity = 8 * ((5 * tok_rows * top_k // (4 * experts) + 7) // 8)
    sliver = width // slivers
    ids_t = expert_ids.T
    order = list(range(experts - 1, 0, -1))
    outs = build(ids_t, tokens, [*order, 0], experts, capacity, sliver)
    built = dict(zip([*order, 0], outs))
    arrived = {s: xor_permute(built[s], "expert", s) for s in order}
    held, sent, kept = first_pass(built[0], w_gate[0], w_up[0], w_down[0], slivers)
    tables = {0: reduce_slivers(sent, kept, slivers)}
    for s in order:
        pieces = gather_slivers(arrived[s], slivers)
        sent, kept = later_pass([pieces], held, slivers)
        tables[s] = xor_permute(reduce_slivers(sent, kept, slivers), "expert", s)
    return combine(ids_t, gate_scores.T, [tables[s] for s in range(experts)])


def solution(mesh):
    in_specs = (
        P(("groups", "expert"), None),
        P(("groups", "expert"), None),
        P(("groups", "expert"), None),
        P("expert", None, "tensor"),
        P("expert", None, "tensor"),
        P("expert", "tensor", None),
    )
    out_specs = P(("groups", "expert"), "tensor")
    return jax.shard_map(
        per_device, mesh=mesh, in_specs=in_specs, out_specs=out_specs, check_vma=False
    )
```

```python
import jax
import jax.numpy as jnp
from jax import lax
from jax.experimental import pallas as pl
from jax.experimental.pallas import tpu as pltpu
from jax.sharding import PartitionSpec as P

F32 = jnp.float32
BF16 = jnp.bfloat16
VMEM = pl.BlockSpec(memory_space=pltpu.VMEM)
HBM = pl.BlockSpec(memory_space=pl.ANY)
BUILD_FLOPS = 50_000_000_000
COST = pl.CostEstimate(flops=1000, bytes_accessed=1000, transcendentals=0)


def params(limit_mib):
    return pltpu.CompilerParams(vmem_limit_bytes=limit_mib << 20)


def xor_permute(value, axis, step):
    size = lax.axis_size(axis)
    return lax.ppermute(value, axis, [(i, i ^ step) for i in range(size)])


def slot_rows(ids_ref, experts, me):
    top_k, rows = ids_ref.shape
    wanted = lax.broadcasted_iota(jnp.int32, (experts, rows), 0) ^ me
    chosen = jnp.zeros((experts, rows), F32)
    for k in range(top_k):
        chosen = chosen + (ids_ref[k : k + 1, :] == wanted).astype(F32)
    earlier = lax.broadcasted_iota(jnp.int32, (rows, rows), 0) < lax.broadcasted_iota(
        jnp.int32, (rows, rows), 1
    )
    before = jnp.dot(
        chosen.astype(BF16), earlier.astype(BF16), preferred_element_type=F32
    )
    return chosen, before


def pick_matrix(chosen, before, step, capacity):
    rows = chosen.shape[1]
    slot = lax.broadcasted_iota(jnp.int32, (capacity, rows), 0).astype(F32)
    hit = (before[step : step + 1, :] == slot) & (chosen[step : step + 1, :] > 0)
    return hit.astype(F32).astype(BF16)


def build_kernel(steps, experts, capacity, ids_ref, tok_ref, *outs):
    me = lax.axis_index("expert")
    own = lax.axis_index("tensor")
    chosen, before = slot_rows(ids_ref, experts, me)
    for step, out in zip(steps, outs):
        matrix = pick_matrix(chosen, before, step, capacity)
        if step == 0:
            moved = jnp.dot(matrix, tok_ref[...], preferred_element_type=F32)
        else:
            sliver = out.shape[1]
            start = pl.multiple_of(own * sliver, 128)
            moved = jnp.dot(
                matrix, tok_ref[:, pl.ds(start, sliver)], preferred_element_type=F32
            )
        out[...] = moved.astype(out.dtype)


def build(ids_t, tokens, steps, experts, capacity, sliver):
    rows, width = tokens.shape
    shapes = [
        jax.ShapeDtypeStruct((capacity, width if s == 0 else sliver), tokens.dtype)
        for s in steps
    ]

    def kernel(*refs):
        build_kernel(steps, experts, capacity, *refs)

    return pl.pallas_call(
        kernel,
        out_shape=shapes,
        in_specs=[VMEM, VMEM],
        out_specs=[VMEM] * len(shapes),
        compiler_params=params(8),
        cost_estimate=pl.CostEstimate(flops=BUILD_FLOPS, bytes_accessed=1000, transcendentals=0),
        name="build_" + "_".join(str(s) for s in steps),
    )(ids_t, tokens)


def down_slivers(hidden, down_ref, sent_ref, kept_ref):
    own = lax.axis_index("tensor")
    half, _, sliver = kept_ref.shape
    for j in range(2 * half):
        start = pl.multiple_of((own ^ j) * sliver, 128)
        part = jnp.dot(hidden, down_ref[:, pl.ds(start, sliver)], preferred_element_type=F32)
        if j % 2 == 1:
            sent_ref[j // 2] = part.astype(BF16)
        else:
            kept_ref[j // 2] = part


def activate(gate, up):
    return (gate / (1.0 + jnp.exp(-gate)) * up).astype(BF16)


def expert_kernel(slivers, chunks, taken, *refs):
    pieces = refs[:taken]
    gate_ref, up_ref, down_ref, sent_ref, kept_ref = refs[taken : taken + 5]
    if chunks:
        lhs = refs[-1]
        own = lax.axis_index("tensor")
        capacity, sliver = pieces[0].shape
        for c in range(chunks):
            for j in range(slivers):
                start = pl.multiple_of((own ^ j) * sliver, 128)
                lhs[pl.ds(c * capacity, capacity), pl.ds(start, sliver)] = pieces[c * slivers + j][...]
    else:
        lhs = pieces[0]
    gate = jnp.dot(lhs[...], gate_ref[...], preferred_element_type=F32)
    up = jnp.dot(lhs[...], up_ref[...], preferred_element_type=F32)
    down_slivers(activate(gate, up), down_ref, sent_ref, kept_ref)


def expert_pass(pieces, weights, slivers):
    if isinstance(pieces, list):
        chunks = len(pieces)
        capacity, sliver = pieces[0][0].shape
        flat = [piece for chunk in pieces for piece in chunk]
        count = chunks * capacity
        scratch = [pltpu.VMEM((count, sliver * slivers), BF16)]
    else:
        chunks = 0
        count, width = pieces.shape
        sliver = width // slivers
        flat = [pieces]
        scratch = []
    half = slivers // 2

    def kernel(*refs):
        expert_kernel(slivers, chunks, len(flat), *refs)

    return pl.pallas_call(
        kernel,
        out_shape=[
            jax.ShapeDtypeStruct((half, count, sliver), BF16),
            jax.ShapeDtypeStruct((half, count, sliver), F32),
        ],
        in_specs=[VMEM] * (len(flat) + 3),
        out_specs=[VMEM] * 2,
        scratch_shapes=scratch,
        compiler_params=params(8),
        cost_estimate=COST,
        name="expert_pass",
    )(*flat, *weights)


def combine_kernel(capacity, ids_ref, score_ref, *refs):
    tables, out_ref = refs[:-1], refs[-1]
    me = lax.axis_index("expert")
    top_k, rows = ids_ref.shape
    experts = len(tables)
    chosen, before = slot_rows(ids_ref, experts, me)
    scores = score_ref[...]
    weights = 2.5 * scores / jnp.sum(scores, axis=0, keepdims=True)
    wanted = lax.broadcasted_iota(jnp.int32, (experts, rows), 0) ^ me
    factor = jnp.zeros((experts, rows), F32)
    for k in range(top_k):
        hit = (ids_ref[k : k + 1, :] == wanted).astype(F32)
        factor = factor + hit * weights[k : k + 1, :]
    factor = factor.T
    total = jnp.zeros(out_ref.shape, F32)
    for step, table in enumerate(tables):
        matrix = pick_matrix(chosen, before, step, capacity)
        picked = lax.dot_general(
            matrix, table[...], (((0,), (0,)), ((), ())), preferred_element_type=F32
        )
        total = total + factor[:, step : step + 1] * picked
    out_ref[...] = total.astype(out_ref.dtype)


def combine(ids_t, scores_t, tables):
    rows = ids_t.shape[1]
    capacity, sliver = tables[0].shape

    def kernel(*refs):
        combine_kernel(capacity, *refs)

    return pl.pallas_call(
        kernel,
        out_shape=jax.ShapeDtypeStruct((rows, sliver), BF16),
        in_specs=[VMEM] * (2 + len(tables)),
        out_specs=VMEM,
        compiler_params=params(8),
        name="combine",
    )(ids_t, scores_t, *tables)


def gather_slivers(piece, slivers):
    held = {0: piece}
    bits = [b for b in range(slivers.bit_length() - 1)]
    for bit in reversed(bits):
        step = 1 << bit
        for j in list(held):
            held[j ^ step] = xor_permute(held[j], "tensor", step)
    return [held[j] for j in range(slivers)]


def reduce_slivers(sent, kept, slivers):
    step = 1
    while True:
        arrived = xor_permute(sent, "tensor", step)
        total = kept + arrived.astype(F32)
        step *= 2
        if step == slivers:
            return total[0].astype(BF16)
        sent = total[1::2].astype(BF16)
        kept = total[0::2]


def per_device(tokens, expert_ids, gate_scores, w_gate, w_up, w_down):
    tok_rows, width = tokens.shape
    top_k = expert_ids.shape[1]
    experts = lax.axis_size("expert")
    slivers = lax.axis_size("tensor")
    capacity = 8 * ((5 * tok_rows * top_k // (4 * experts) + 7) // 8)
    sliver = width // slivers
    ids_t = expert_ids.T
    order = list(range(experts - 1, 0, -1))
    outs = build(ids_t, tokens, [*order, 0], experts, capacity, sliver)
    built = dict(zip([*order, 0], outs))
    arrived = {s: xor_permute(built[s], "expert", s) for s in order}
    weights = (w_gate[0], w_up[0], w_down[0])
    sent, kept = expert_pass(built[0], weights, slivers)
    tables = {0: reduce_slivers(sent, kept, slivers)}
    for s in order:
        pieces = gather_slivers(arrived[s], slivers)
        sent, kept = expert_pass([pieces], weights, slivers)
        tables[s] = xor_permute(reduce_slivers(sent, kept, slivers), "expert", s)
    return combine(ids_t, gate_scores.T, [tables[s] for s in range(experts)])


def solution(mesh):
    in_specs = (
        P(("groups", "expert"), None),
        P(("groups", "expert"), None),
        P(("groups", "expert"), None),
        P("expert", None, "tensor"),
        P("expert", None, "tensor"),
        P("expert", "tensor", None),
    )
    out_specs = P(("groups", "expert"), "tensor")
    return jax.shard_map(
        per_device, mesh=mesh, in_specs=in_specs, out_specs=out_specs, check_vma=False
    )
```
